32 devices in a mesh: row: 8 (over z, y), col: 4 (over x, core).
Axes of the slice: x: 2, y: 2, z: 4, core: 2. Of those that a mesh axis runs over, the one named last changes fastest.
Arguments:
- weights: bfloat16 [2, 8192, 8192], P(None, 'row', 'col'), may hold values from -0.0625 to 0.0625
- preact: float32 [2, 2, 8192], P(None, None, 'row'), may hold values from -2.5 to 2.5
- panel: bfloat16 [2, 64, 8192], P(None, None, 'col'), may hold values from -6 to 6
Outputs:
- basis_out: float32 [2, 64, 8192], P(None, None, 'col')
The draws below stay inside these ranges and needn't reach their ends.
All inputs are finite; a program needn't handle non-finite values.
Results may differ from the reference program's by a relative error of at most 0.035.
Values may be sent and summed in bfloat16 or wider, within the bound.
A program may use at most 64 MiB of HBM per device.

```python
from functools import partial
import jax
import jax.numpy as jnp
from jax import lax

WIDTH = 8192
RANK = 64
LAYERS = 2
ITERS = 2
INPUTS = 2
N_ROW = 8
N_COL = 4


def block_levels(key, shape, split, low, top_value):
    def one(position, parts):
        draws = jax.random.uniform(jax.random.fold_in(jax.random.fold_in(key, 6), position), (parts,), jnp.float32, low / len(split), top_value / len(split))
        return jnp.repeat(jnp.exp(draws), shape[position] // parts).reshape((-1,) + (1,) * (len(shape) - position - 1))

    gain = one(*split[0])
    for cut in split[1:]:
        gain = gain * one(*cut)
    return gain


def scatter_about(key, shape, spread, most, shards=(), held_as=jnp.bfloat16):
    factor_of = block_levels(key, shape, shards, -0.22, 0.18) if shards else 1.0
    drawn = jax.random.normal(key, shape, jnp.float32) * spread * factor_of
    return jnp.minimum(jnp.maximum(drawn, -most), most).astype(held_as)


def setup_inputs(seed: int = 0) -> dict:
    keys = jax.random.split(jax.random.key(seed), 4)
    return {
        "weights": scatter_about(keys[0], (LAYERS, WIDTH, WIDTH), WIDTH ** -0.5, 0.0625, ((1, 8), (2, 4))),
        "preact": scatter_about(keys[1], (INPUTS, LAYERS, WIDTH), 0.8, 2.5, ((2, 8),), jnp.float32),
        "panel": scatter_about(keys[2], (INPUTS, RANK, WIDTH), 1.0, 6.0, ((2, 4),)),
    }


def forward_layer(values, weight):
    inputs, rows, width = values.shape
    blocks = values.astype(jnp.float32).reshape(inputs, rows, N_COL, width // N_COL)
    weight_blocks = weight.astype(jnp.float32).reshape(width, N_COL, width // N_COL)
    partials = jnp.einsum('bkci,oci->cbko', blocks, weight_blocks, precision=lax.Precision.HIGHEST)
    rounded = lax.optimization_barrier(partials.astype(jnp.bfloat16))
    return jnp.sum(rounded.astype(jnp.float32), axis=0)

def backward_layer(values, weight):
    inputs, rows, width = values.shape
    blocks = values.astype(jnp.float32).reshape(inputs, rows, N_ROW, width // N_ROW)
    weight_blocks = weight.astype(jnp.float32).reshape(N_ROW, width // N_ROW, width)
    partials = jnp.einsum('bkro,roi->rbki', blocks, weight_blocks, precision=lax.Precision.HIGHEST)
    rounded = lax.optimization_barrier(partials.astype(jnp.bfloat16))
    return jnp.sum(rounded.astype(jnp.float32), axis=0)

def reference(weights, preact, panel):
    slopes = 1.0 - jnp.tanh(preact) ** 2
    current = panel
    basis_out = panel.astype(jnp.float32)
    for iteration in range(ITERS):
        forward = current
        for layer_at in range(LAYERS):
            summed = forward_layer(forward, weights[layer_at])
            forward = (slopes[:, layer_at, None, :] * summed).astype(jnp.bfloat16)
        cotangent = forward
        for layer_at in reversed(range(LAYERS)):
            weighted = (slopes[:, layer_at, None, :] * cotangent.astype(jnp.float32)).astype(jnp.bfloat16)
            cotangent = backward_layer(weighted, weights[layer_at]).astype(jnp.bfloat16)
        image_panel = cotangent.astype(jnp.float32)
        gram_sum = jnp.einsum('bkw,bjw->bkj', image_panel, image_panel, precision=lax.Precision.HIGHEST)
        factor = jnp.linalg.cholesky(gram_sum / WIDTH)
        basis_out = jax.vmap(partial(jax.scipy.linalg.solve_triangular, lower=True))(factor, image_panel)
        current = basis_out.astype(jnp.bfloat16)
    return basis_out
```

```python
from functools import partial

import jax
import jax.numpy as jnp
from jax import lax
from jax.experimental import pallas as pl
from jax.experimental.pallas import tpu as pltpu
from jax.sharding import PartitionSpec as P

ITERS = 2
MESH = pl.DeviceIdType.MESH
F32, BF16 = jnp.float32, jnp.bfloat16


def plain_on_device(weights, preact, panel):
    width = panel.shape[2] * lax.axis_size("col")
    slopes = 1.0 - jnp.tanh(preact) ** 2
    layers = weights.shape[0]
    current = panel
    basis_out = panel.astype(F32)
    for iteration in range(ITERS):
        cotangent = None
        for layer_at in range(layers):
            partial_out = jnp.einsum("bki,oi->bko", current, weights[layer_at], preferred_element_type=F32)
            summed = lax.psum_scatter(
                partial_out.astype(BF16), "col", scatter_dimension=1, tiled=True
            ).astype(F32)
            scaled = (slopes[:, layer_at, None, :] * summed).astype(BF16)
            if layer_at + 1 < layers:
                spread = lax.all_gather(scaled, "row", axis=2, tiled=True)
                current = lax.all_to_all(spread, "col", split_axis=2, concat_axis=1, tiled=True)
            else:
                cotangent = lax.all_gather(scaled, "col", axis=1, tiled=True)
        image_panel = None
        for layer_at in reversed(range(layers)):
            weighted = (slopes[:, layer_at, None, :] * cotangent).astype(BF16)
            partial_in = jnp.einsum("bko,oi->bki", weighted, weights[layer_at], preferred_element_type=F32)
            if layer_at == 0:
                pieces = lax.psum_scatter(partial_in.astype(BF16), "row", scatter_dimension=2, tiled=True)
                image_panel = lax.all_gather(pieces, "row", axis=2, tiled=True)
            else:
                pieces = lax.psum_scatter(partial_in.astype(BF16), "row", scatter_dimension=1, tiled=True)
                spread = lax.all_gather(pieces, "col", axis=2, tiled=True)
                cotangent = lax.all_to_all(spread, "row", split_axis=2, concat_axis=1, tiled=True)
        local_gram = jnp.einsum("bkw,bjw->bkj", image_panel, image_panel, preferred_element_type=F32)
        gram_sum = lax.psum(local_gram.astype(BF16), "col").astype(F32)
        factor = jnp.linalg.cholesky(gram_sum / width)
        basis_out = jax.vmap(partial(jax.scipy.linalg.solve_triangular, lower=True))(
            factor, image_panel.astype(F32)
        )
        current = basis_out.astype(BF16)
    return basis_out


def inverse_factors(gram, inputs, rank, width):
    at_row = lax.broadcasted_iota(jnp.int32, (rank, 1), 0)
    row_at = lax.broadcasted_iota(jnp.int32, (rank, rank), 0)
    col_at = lax.broadcasted_iota(jnp.int32, (rank, rank), 1)
    eye = (row_at == col_at).astype(F32)
    joined = [
        jnp.concatenate([gram[:, b * rank:(b + 1) * rank], eye], axis=1) for b in range(inputs)
    ]
    for k in range(rank):
        for b in range(inputs):
            now = joined[b]
            pivot_row = now[k:k + 1, :]
            share = now[:, k:k + 1] / now[k:k + 1, k:k + 1]
            joined[b] = now - jnp.where(at_row > k, share, 0.0) * pivot_row
    inverses = []
    for b in range(inputs):
        diagonal = jnp.sum(joined[b][:, :rank] * eye, axis=1, keepdims=True)
        inverses.append(joined[b][:, rank:] * jnp.sqrt(width / diagonal))
    return inverses


def apply_inverse(inverse, panel):
    high = inverse.astype(BF16)
    low = (inverse - high.astype(F32)).astype(BF16)
    return jnp.dot(high, panel, preferred_element_type=F32) + jnp.dot(low, panel, preferred_element_type=F32)


def kernel(
    rows, cols, inputs, rank, out_block, in_block,
    w_hbm, preact_ref, panel_ref, out_ref,
    w, slopes, part_col, got_col, ring, spread, gathered_col, part_in, traded, sums,
    part_row, got_row, image, gram, w_sem, col_send, col_recv, row_send, row_recv,
    fwd_send, fwd_recv, sum_send, sum_recv,
):
    r, c = lax.axis_index("row"), lax.axis_index("col")
    n = inputs * rank
    layers = w.shape[0]
    per = rows // cols
    n_col, n_row = n // cols, n // rows
    width = cols * in_block
    per_input = cols // inputs
    my_input = c // per_input
    tile = 256

    loads = [pltpu.make_async_copy(w_hbm.at[l], w.at[l], w_sem.at[l]) for l in range(layers)]
    for load in loads:
        load.start()
    barrier = pltpu.get_barrier_semaphore()
    for d in range(1, rows):
        pl.semaphore_signal(barrier, inc=1, device_id={"row": lax.rem(r + d, rows)}, device_id_type=MESH)
    for d in range(1, cols):
        pl.semaphore_signal(barrier, inc=1, device_id={"col": lax.rem(c + d, cols)}, device_id_type=MESH)
    slopes[...] = 1.0 - jnp.tanh(preact_ref[...]) ** 2
    pl.semaphore_wait(barrier, rows + cols - 2)

    pending = []

    def trade(axis, source_of, into, send, recv):
        me, size = (r, rows) if axis == "row" else (c, cols)
        for d in range(1, size):
            peer = lax.rem(me + d, size)
            copy = pltpu.make_async_remote_copy(
                src_ref=source_of(peer), dst_ref=into.at[me], send_sem=send.at[d], recv_sem=recv.at[d],
                device_id={axis: peer}, device_id_type=MESH)
            copy.start()
            pending.append((None, copy))

        def arrive(d):
            origin = lax.rem(me + size - d, size)
            pltpu.make_async_remote_copy(
                src_ref=source_of(origin), dst_ref=into.at[origin], send_sem=send.at[d], recv_sem=recv.at[d],
                device_id={axis: origin}, device_id_type=MESH).wait_recv()
            return origin

        return arrive

    def forward(layer, pieces, into):
        def step(t, carry):
            at = pl.ds(pl.multiple_of(t * tile, tile), tile)
            total = None
            for lhs, low, high in pieces():
                term = lax.dot_general(
                    lhs, w[layer, at, low:high], (((1,), (1,)), ((), ())), preferred_element_type=F32)
                total = term if total is None else total + term
            into[:, :, at] = total.astype(BF16).reshape(cols, n_col, tile)
            return carry
        lax.fori_loop(0, out_block // tile, step, 0)

    def backward(layer, lhs_ref, store):
        def step(t, carry):
            at = pl.ds(pl.multiple_of(t * tile, tile), tile)
            store(t, jnp.dot(lhs_ref[...], w[layer, :, at], preferred_element_type=F32).astype(BF16))
            return carry
        lax.fori_loop(0, in_block // tile, step, 0)

    def weigh(layer, values_of, into):
        for b in range(inputs):
            into[b * rank:(b + 1) * rank, :] = (
                slopes[b * layers + layer:b * layers + layer + 1, :] * values_of(b)
            ).astype(BF16)

    def gathered_input(buf, b):
        return buf[b * per_input:(b + 1) * per_input].reshape(rank, out_block)

    def reduce_col(it, slot, part, got):
        arrive = trade("col", lambda peer: part.at[peer], got, col_send.at[it, slot], col_recv.at[it, slot])
        total = part[c].astype(F32)
        for d in range(1, cols):
            total = total + got[arrive(d)].astype(F32)
        return total

    def gather_col(it, slot, value, buf):
        buf[c] = value
        arrive = trade("col", lambda peer: buf.at[c], buf, col_send.at[it, slot], col_recv.at[it, slot])
        for d in range(1, cols):
            arrive(d)

    def factors(it):
        total = gram[it, 0]
        for at in range(1, cols):
            total = total + gram[it, at]
        return inverse_factors(total, inputs, rank, float(width))

    weighted = part_in.at[0]
    gram_arrive = None
    inverses = None
    for it in range(ITERS):
        first = panel_ref if it == 0 else None
        if it == 0:
            loads[0].wait()
        lhs = (lambda: [(panel_ref[...], 0, in_block)]) if it == 0 else (
            lambda: [(image[it - 1].reshape(n, in_block), 0, in_block)])
        for layer in range(layers):
            if it == 0 and layer > 0:
                loads[layer].wait()
            forward(layer, lhs, part_col.at[it, layer])
            summed = reduce_col(it, layer, part_col.at[it, layer], got_col.at[it, layer])
            my_slope = slopes[pl.ds(my_input * layers + layer, 1), :]
            if layer + 1 < layers:
                shards = ring.at[it, layer]
                shards[r] = (my_slope * summed).astype(BF16)
                arrive = trade("row", lambda peer: shards.at[r], shards,
                               row_send.at[it, layer], row_recv.at[it, layer])
                if it > 0 and layer == 0:
                    for d in range(1, cols):
                        gram_arrive(d)
                    inverses = factors(it - 1)
                blocks = spread.at[it, layer]
                for d in range(rows):
                    origin = arrive(d) if d else r
                    owner, at = origin // per, lax.rem(origin, per)
                    copy = pltpu.make_async_remote_copy(
                        src_ref=shards.at[origin], dst_ref=blocks.at[at, c],
                        send_sem=fwd_send.at[it, layer, d], recv_sem=fwd_recv.at[it, layer, at, c],
                        device_id={"col": owner}, device_id_type=MESH)

                    @pl.when(owner != c)
                    def _():
                        copy.start()

                    @pl.when(owner == c)
                    def _():
                        blocks[at, c] = shards[origin]
                    pending.append((owner != c, copy))
                for at in range(per):
                    for d in range(1, cols):
                        origin = lax.rem(c + d, cols)
                        pltpu.make_async_remote_copy(
                            src_ref=blocks.at[at, origin], dst_ref=blocks.at[at, origin],
                            send_sem=fwd_send.at[it, layer, 0], recv_sem=fwd_recv.at[it, layer, at, origin],
                            device_id={"col": origin}, device_id_type=MESH).wait_recv()
                lhs = lambda blocks=blocks: [
                    (blocks[at].reshape(n, out_block), at * out_block, (at + 1) * out_block) for at in range(per)]
            else:
                cot = gathered_col.at[it, layer]
                gather_col(it, layers, ((my_slope * summed) if it == 0 else summed).astype(BF16), cot)
        left = part_in.at[it]
        for layer in reversed(range(layers)):
            scaled = sums.at[it, layer]
            if layer == layers - 1 and it > 0:
                def values_of(b):
                    mixed = apply_inverse(inverses[b], gathered_input(cot, b))
                    slope = slopes[b * layers + layer:b * layers + layer + 1, :]
                    return (slope * mixed).astype(BF16).astype(F32)
            else:
                def values_of(b):
                    return gathered_input(cot, b).astype(F32)
            weigh(layer, values_of, scaled)
            if layer > 0:
                def store(t, value):
                    ratio = out_block // tile
                    at = pl.ds(pl.multiple_of(lax.rem(t, ratio) * tile, tile), tile)
                    left[layer, :, t // ratio, :, at] = value.reshape(cols, n_col, tile)
                backward(layer, scaled, store)
                whole = traded.at[it, layer, 0]
                got = traded.at[it, layer, 1]
                source = left.at[layer]
                arrive = trade("col", lambda peer: source.at[peer], whole,
                               col_send.at[it, layers + layer], col_recv.at[it, layers + layer])
                whole[c] = source[c]
                into = ring.at[it, layers - 1 + layer - 1] if False else got
                slots = into
                for d in range(cols):
                    owner = arrive(d) if d else c
                    for at in range(per):
                        target = owner * per + at
                        copy = pltpu.make_async_remote_copy(
                            src_ref=whole.at[owner, at],
                            dst_ref=slots.at[r // per, lax.rem(r, per)],
                            send_sem=sum_send.at[it, layer, d * per + at], recv_sem=sum_recv.at[it, layer, r],
                            device_id={"row": target}, device_id_type=MESH)

                        @pl.when(target != r)
                        def _():
                            copy.start()
                        pending.append((target != r, copy))
                total = whole[r // per, lax.rem(r, per)].astype(F32)
                for d in range(1, rows):
                    origin = lax.rem(r + d, rows)
                    place = slots.at[origin // per, lax.rem(origin, per)]
                    pltpu.make_async_remote_copy(
                        src_ref=place, dst_ref=place, send_sem=sum_send.at[it, layer, 0],
                        recv_sem=sum_recv.at[it, layer, origin],
                        device_id={"row": origin}, device_id_type=MESH).wait_recv()
                    total = total + place[...].astype(F32)
                cot = gathered_col.at[it, layer - 1]
                gather_col(it, 2 * layers + layer - 1, total.astype(BF16), cot)
            else:
                mine = part_row.at[it]

                def store(t, value):
                    mine[:, :, pl.ds(pl.multiple_of(t * tile, tile), tile)] = value.reshape(rows, n_row, tile)
                backward(layer, scaled, store)
                got = got_row.at[it]
                arrive = trade("row", lambda peer: mine.at[peer], got,
                               row_send.at[it, layers], row_recv.at[it, layers])
                total = mine[r].astype(F32)
                for d in range(1, rows):
                    total = total + got[arrive(d)].astype(F32)
                final = image.at[it]
                final[r] = total.astype(BF16)
                arrive = trade("row", lambda peer: final.at[r], final,
                               row_send.at[it, layers + 1], row_recv.at[it, layers + 1])
                for d in range(1, rows):
                    arrive(d)
        half = rows // inputs
        local = []
        for b in range(inputs):
            own = image[it, b * half:(b + 1) * half].reshape(rank, in_block)
            local.append(lax.dot_general(own, own, (((1,), (1,)), ((), ())), preferred_element_type=F32))
        gram[it, c] = jnp.concatenate(local, axis=1)
        here = gram.at[it]
        gram_arrive = trade("col", lambda peer, here=here: here.at[c], here,
                            col_send.at[it, 3 * layers], col_recv.at[it, 3 * layers])
    for d in range(1, cols):
        gram_arrive(d)
    inverses = factors(ITERS - 1)
    half = rows // inputs
    for b in range(inputs):
        own = image[ITERS - 1, b * half:(b + 1) * half].reshape(rank, in_block)
        out_ref[b * rank:(b + 1) * rank, :] = apply_inverse(inverses[b], own)
    for condition, copy in pending:
        if condition is None:
            copy.wait_send()
        else:
            @pl.when(condition)
            def _():
                copy.wait_send()


def on_device(rows, cols, weights, preact, panel):
    layers, out_block, in_block = weights.shape
    inputs, rank, _ = panel.shape
    n = inputs * rank
    per = rows // cols
    vm = pltpu.VMEM
    dma = pltpu.SemaphoreType.DMA
    scratch = [
        vm((layers, out_block, in_block), BF16),
        vm((inputs * layers, out_block), F32),
        vm((ITERS, layers, cols, n // cols, out_block), BF16),
        vm((ITERS, layers, cols, n // cols, out_block), BF16),
        vm((ITERS, layers - 1, rows, n // cols, out_block), BF16),
        vm((ITERS, layers - 1, per, cols, n // cols, out_block), BF16),
        vm((ITERS, layers, cols, n // cols, out_block), BF16),
        vm((ITERS, layers, cols, per, n // cols, out_block), BF16),
        vm((ITERS, layers, 2, cols, per, n // cols, out_block), BF16),
        vm((ITERS, layers, n, out_block), BF16),
        vm((ITERS, rows, n // rows, in_block), BF16),
        vm((ITERS, rows, n // rows, in_block), BF16),
        vm((ITERS, rows, n // rows, in_block), BF16),
        vm((ITERS, cols, rank, inputs * rank), F32),
        dma((layers,)),
        dma((ITERS, 3 * layers + 1, cols)), dma((ITERS, 3 * layers + 1, cols)),
        dma((ITERS, layers + 2, rows)), dma((ITERS, layers + 2, rows)),
        dma((ITERS, layers, rows)), dma((ITERS, layers, per, cols)),
        dma((ITERS, layers, rows)), dma((ITERS, layers, rows)),
    ]
    whole = pl.BlockSpec(memory_space=pltpu.VMEM)
    out = pl.pallas_call(
        partial(kernel, rows, cols, inputs, rank, out_block, in_block),
        out_shape=jax.ShapeDtypeStruct((n, in_block), F32),
        in_specs=[pl.BlockSpec(memory_space=pl.ANY), whole, whole],
        out_specs=whole,
        scratch_shapes=scratch,
        compiler_params=pltpu.CompilerParams(
            collective_id=0, has_side_effects=True, vmem_limit_bytes=56 * 1024 * 1024),
    )(weights, preact.reshape(inputs * layers, out_block), panel.reshape(n, in_block))
    return out.reshape(inputs, rank, in_block)


def solution(mesh):
    rows, cols = mesh.shape["row"], mesh.shape["col"]

    def body(weights, preact, panel):
        layers, out_block, in_block = weights.shape
        inputs, rank, _ = panel.shape
        n = inputs * rank
        fits = (
            rows % cols == 0 and cols % inputs == 0 and rows % inputs == 0
            and n % (16 * rows) == 0 and n % (16 * cols) == 0
            and out_block % 256 == 0 and rows * out_block == cols * in_block
        )
        if fits:
            return on_device(rows, cols, weights, preact, panel)
        return plain_on_device(weights, preact, panel)

    return jax.shard_map(
        body,
        mesh=mesh,
        in_specs=(P(None, "row", "col"), P(None, None, "row"), P(None, None, "col")),
        out_specs=P(None, None, "col"),
        check_vma=False,
    )
```

```python
from functools import partial

import jax
import jax.numpy as jnp
from jax import lax
from jax.experimental import pallas as pl
from jax.experimental.pallas import tpu as pltpu
from jax.sharding import PartitionSpec as P

ITERS = 2
MESH = pl.DeviceIdType.MESH
F32, BF16 = jnp.float32, jnp.bfloat16


def plain_on_device(weights, preact, panel):
    width = panel.shape[2] * lax.axis_size("col")
    slopes = 1.0 - jnp.tanh(preact) ** 2
    layers = weights.shape[0]
    current = panel
    basis_out = panel.astype(F32)
    for iteration in range(ITERS):
        cotangent = None
        for layer_at in range(layers):
            partial_out = jnp.einsum("bki,oi->bko", current, weights[layer_at], preferred_element_type=F32)
            summed = lax.psum_scatter(
                partial_out.astype(BF16), "col", scatter_dimension=1, tiled=True
            ).astype(F32)
            scaled = (slopes[:, layer_at, None, :] * summed).astype(BF16)
            if layer_at + 1 < layers:
                spread = lax.all_gather(scaled, "row", axis=2, tiled=True)
                current = lax.all_to_all(spread, "col", split_axis=2, concat_axis=1, tiled=True)
            else:
                cotangent = lax.all_gather(scaled, "col", axis=1, tiled=True)
        image_panel = None
        for layer_at in reversed(range(layers)):
            weighted = (slopes[:, layer_at, None, :] * cotangent).astype(BF16)
            partial_in = jnp.einsum("bko,oi->bki", weighted, weights[layer_at], preferred_element_type=F32)
            if layer_at == 0:
                pieces = lax.psum_scatter(partial_in.astype(BF16), "row", scatter_dimension=2, tiled=True)
                image_panel = lax.all_gather(pieces, "row", axis=2, tiled=True)
            else:
                pieces = lax.psum_scatter(partial_in.astype(BF16), "row", scatter_dimension=1, tiled=True)
                spread = lax.all_gather(pieces, "col", axis=2, tiled=True)
                cotangent = lax.all_to_all(spread, "row", split_axis=2, concat_axis=1, tiled=True)
        local_gram = jnp.einsum("bkw,bjw->bkj", image_panel, image_panel, preferred_element_type=F32)
        gram_sum = lax.psum(local_gram.astype(BF16), "col").astype(F32)
        factor = jnp.linalg.cholesky(gram_sum / width)
        basis_out = jax.vmap(partial(jax.scipy.linalg.solve_triangular, lower=True))(
            factor, image_panel.astype(F32)
        )
        current = basis_out.astype(BF16)
    return basis_out


def inverse_factors(gram, inputs, rank, width):
    at_row = lax.broadcasted_iota(jnp.int32, (rank, 1), 0)
    row_at = lax.broadcasted_iota(jnp.int32, (rank, rank), 0)
    col_at = lax.broadcasted_iota(jnp.int32, (rank, rank), 1)
    eye = (row_at == col_at).astype(F32)
    joined = [
        jnp.concatenate([gram[:, b * rank:(b + 1) * rank], eye], axis=1) for b in range(inputs)
    ]
    for k in range(rank):
        for b in range(inputs):
            now = joined[b]
            pivot_row = now[k:k + 1, :]
            share = now[:, k:k + 1] / now[k:k + 1, k:k + 1]
            joined[b] = now - jnp.where(at_row > k, share, 0.0) * pivot_row
    inverses = []
    for b in range(inputs):
        diagonal = jnp.sum(joined[b][:, :rank] * eye, axis=1, keepdims=True)
        inverses.append(joined[b][:, rank:] * jnp.sqrt(width / diagonal))
    return inverses


def apply_inverse(inverse, panel):
    high = inverse.astype(BF16)
    low = (inverse - high.astype(F32)).astype(BF16)
    return jnp.dot(high, panel, preferred_element_type=F32) + jnp.dot(low, panel, preferred_element_type=F32)


def kernel(
    rows, cols, inputs, rank, out_block, in_block, slices,
    w_hbm, preact_ref, panel_ref, out_ref,
    w, slopes, part_col, got_col, ring, spread, gathered_col, part_in, traded, summed_in, weighted,
    part_row, got_row, image, gram, w_sem, col_send, col_recv, row_send, row_recv,
    fwd_send, fwd_recv, sum_send, sum_recv,
):
    r, c = lax.axis_index("row"), lax.axis_index("col")
    layers = w.shape[0]
    per = rows // cols
    k_col, k_row = rank // cols, rank // slices
    pieces = rows // slices
    piece = in_block // pieces
    width = cols * in_block
    tile = 256

    loads = [pltpu.make_async_copy(w_hbm.at[l], w.at[l], w_sem.at[l]) for l in range(layers)]
    for load in loads:
        load.start()
    barrier = pltpu.get_barrier_semaphore()
    for d in range(1, rows):
        pl.semaphore_signal(barrier, inc=1, device_id={"row": lax.rem(r + d, rows)}, device_id_type=MESH)
    for d in range(1, cols):
        pl.semaphore_signal(barrier, inc=1, device_id={"col": lax.rem(c + d, cols)}, device_id_type=MESH)
    slopes[...] = 1.0 - jnp.tanh(preact_ref[...]) ** 2
    pl.semaphore_wait(barrier, rows + cols - 2)

    pending = []
    loaded = set()
    gram_arrivals = []
    inverses = {}

    def need(layer):
        if layer not in loaded:
            loaded.add(layer)
            loads[layer].wait()

    def trade(axis, source_of, place_of, send, recv):
        me, size = (r, rows) if axis == "row" else (c, cols)
        for d in range(1, size):
            peer = lax.rem(me + d, size)
            copy = pltpu.make_async_remote_copy(
                src_ref=source_of(peer), dst_ref=place_of(me), send_sem=send.at[d], recv_sem=recv.at[d],
                device_id={axis: peer}, device_id_type=MESH)
            copy.start()
            pending.append((None, copy))

        def arrive(d):
            origin = lax.rem(me + size - d, size)
            pltpu.make_async_remote_copy(
                src_ref=source_of(origin), dst_ref=place_of(origin), send_sem=send.at[d], recv_sem=recv.at[d],
                device_id={axis: origin}, device_id_type=MESH).wait_recv()
            return origin

        return arrive

    def forward(layer, lhs, into):
        need(layer)

        def step(t, carry):
            at = pl.ds(pl.multiple_of(t * tile, tile), tile)
            total = None
            for value, low, high in lhs():
                term = lax.dot_general(
                    value, w[layer, at, low:high], (((1,), (1,)), ((), ())), preferred_element_type=F32)
                total = term if total is None else total + term
            into[:, :, at] = total.astype(BF16).reshape(cols, k_col, tile)
            return carry
        lax.fori_loop(0, out_block // tile, step, 0)

    def backward(layer, lhs_ref, store):
        def step(t, carry):
            at = pl.ds(pl.multiple_of(t * tile, tile), tile)
            store(t, jnp.dot(lhs_ref[...], w[layer, :, at], preferred_element_type=F32).astype(BF16))
            return carry
        lax.fori_loop(0, in_block // tile, step, 0)

    def stream(b):
        for it in range(ITERS):
            if it == 0:
                lhs = lambda: [(panel_ref[b * rank:(b + 1) * rank, :], 0, in_block)]
            else:
                lhs = lambda: [
                    (image[b, it - 1, h].reshape(rank, piece), h * piece, (h + 1) * piece) for h in range(pieces)]
            for layer in range(layers):
                slope = slopes[b * layers + layer:b * layers + layer + 1, :]
                part, got = part_col.at[b, it, layer], got_col.at[b, it, layer]
                forward(layer, lhs, part)
                arrive = trade("col", lambda peer: part.at[peer], lambda me: got.at[me],
                               col_send.at[b, it, layer], col_recv.at[b, it, layer])
                yield
                total = part[c].astype(F32)
                for d in range(1, cols):
                    total = total + got[arrive(d)].astype(F32)
                if layer + 1 < layers:
                    shards, blocks = ring.at[b, it, layer], spread.at[b, it, layer]
                    shards[r] = (slope * total).astype(BF16)
                    arrive = trade("row", lambda peer: shards.at[r], lambda me: shards.at[me],
                                   row_send.at[b, it, layer], row_recv.at[b, it, layer])
                    if it > 0 and layer == 0 and b == inputs - 1:
                        finish_grams(it - 1)
                    yield
                    for d in range(rows):
                        origin = arrive(d) if d else r
                        owner, at = origin // per, lax.rem(origin, per)
                        copy = pltpu.make_async_remote_copy(
                            src_ref=shards.at[origin], dst_ref=blocks.at[at, c],
                            send_sem=fwd_send.at[b, it, layer, d], recv_sem=fwd_recv.at[b, it, layer, at, c],
                            device_id={"col": owner}, device_id_type=MESH)

                        @pl.when(owner != c)
                        def _():
                            copy.start()

                        @pl.when(owner == c)
                        def _():
                            blocks[at, c] = shards[origin]
                        pending.append((owner != c, copy))
                    yield
                    for at in range(per):
                        for d in range(1, cols):
                            origin = lax.rem(c + d, cols)
                            pltpu.make_async_remote_copy(
                                src_ref=blocks.at[at, origin], dst_ref=blocks.at[at, origin],
                                send_sem=fwd_send.at[b, it, layer, 0], recv_sem=fwd_recv.at[b, it, layer, at, origin],
                                device_id={"col": origin}, device_id_type=MESH).wait_recv()
                    lhs = lambda blocks=blocks: [
                        (blocks[at].reshape(rank, out_block), at * out_block, (at + 1) * out_block)
                        for at in range(per)]
                else:
                    cot = gathered_col.at[b, it, layer]
                    cot[c] = ((slope * total) if it == 0 else total).astype(BF16)
                    arrive = trade("col", lambda peer: cot.at[c], lambda me: cot.at[me],
                                   col_send.at[b, it, layers], col_recv.at[b, it, layers])
                    yield
                    for d in range(1, cols):
                        arrive(d)
            for layer in reversed(range(layers)):
                slope = slopes[b * layers + layer:b * layers + layer + 1, :]
                scaled = weighted.at[b, it, layer]
                value = cot[...].reshape(rank, out_block)
                if layer == layers - 1 and it > 0:
                    value = (slope * apply_inverse(inverses[it - 1][b], value)).astype(BF16)
                scaled[...] = (slope * value.astype(F32)).astype(BF16)
                if layer > 0:
                    whole, slots = traded.at[b, it, layer], summed_in.at[b, it, layer]
                    source = part_in.at[b, it, layer]

                    def store(t, value):
                        ratio = out_block // tile
                        at = pl.ds(pl.multiple_of(lax.rem(t, ratio) * tile, tile), tile)
                        source[:, t // ratio, :, at] = value.reshape(cols, k_col, tile)
                    backward(layer, scaled, store)
                    arrive = trade("col", lambda peer: source.at[peer], lambda me: whole.at[me],
                                   col_send.at[b, it, layers + layer], col_recv.at[b, it, layers + layer])
                    whole[c] = source[c]
                    yield
                    for d in range(cols):
                        owner = arrive(d) if d else c
                        for at in range(per):
                            target = owner * per + at
                            copy = pltpu.make_async_remote_copy(
                                src_ref=whole.at[owner, at], dst_ref=slots.at[r],
                                send_sem=sum_send.at[b, it, layer, d * per + at], recv_sem=sum_recv.at[b, it, layer, r],
                                device_id={"row": target}, device_id_type=MESH)

                            @pl.when(target != r)
                            def _():
                                copy.start()
                            pending.append((target != r, copy))
                    yield
                    total = whole[r // per, lax.rem(r, per)].astype(F32)
                    for d in range(1, rows):
                        origin = lax.rem(r + d, rows)
                        place = slots.at[origin]
                        pltpu.make_async_remote_copy(
                            src_ref=place, dst_ref=place, send_sem=sum_send.at[b, it, layer, 0],
                            recv_sem=sum_recv.at[b, it, layer, origin],
                            device_id={"row": origin}, device_id_type=MESH).wait_recv()
                        total = total + place[...].astype(F32)
                    cot = gathered_col.at[b, it, layer - 1]
                    cot[c] = total.astype(BF16)
                    arrive = trade("col", lambda peer: cot.at[c], lambda me: cot.at[me],
                                   col_send.at[b, it, 2 * layers + layer - 1],
                                   col_recv.at[b, it, 2 * layers + layer - 1])
                    yield
                    for d in range(1, cols):
                        arrive(d)
                else:
                    mine, got, final = part_row.at[b, it], got_row.at[b, it], image.at[b, it]

                    def store(t, value):
                        ratio = piece // tile
                        at = pl.ds(pl.multiple_of(lax.rem(t, ratio) * tile, tile), tile)
                        mine[t // ratio, :, :, at] = value.reshape(slices, k_row, tile)
                    backward(layer, scaled, store)

                    def shard(ref):
                        return lambda at: ref.at[at // slices, lax.rem(at, slices)]
                    arrive = trade("row", shard(mine), shard(got), row_send.at[b, it, layers], row_recv.at[b, it, layers])
                    yield
                    total = shard(mine)(r)[...].astype(F32)
                    for d in range(1, rows):
                        total = total + shard(got)(arrive(d))[...].astype(F32)
                    shard(final)(r)[...] = total.astype(BF16)
                    arrive = trade("row", lambda peer: shard(final)(r), shard(final),
                                   row_send.at[b, it, layers + 1], row_recv.at[b, it, layers + 1])
                    yield
                    for d in range(1, rows):
                        arrive(d)
            local = None
            for h in range(pieces):
                own = image[b, it, h].reshape(rank, piece)
                term = lax.dot_general(own, own, (((1,), (1,)), ((), ())), preferred_element_type=F32)
                local = term if local is None else local + term
            here = gram.at[b, it]
            here[c] = jnp.concatenate([local, local], axis=1)
            gram_arrivals.append((it, b, trade(
                "col", lambda peer, here=here: here.at[c], lambda me, here=here: here.at[me],
                col_send.at[b, it, 3 * layers], col_recv.at[b, it, 3 * layers])))

    def finish_grams(it):
        totals = {}
        for at, b, arrive in gram_arrivals:
            if at == it:
                for d in range(1, cols):
                    arrive(d)
                total = gram[b, it, 0]
                for d in range(1, cols):
                    total = total + gram[b, it, d]
                totals[b] = total[:, :rank]
        joint = jnp.concatenate([totals[b] for b in range(inputs)], axis=1)
        inverses[it] = inverse_factors(joint, inputs, rank, float(width))

    running = [stream(b) for b in range(inputs)]
    while running:
        for chain in list(running):
            try:
                next(chain)
            except StopIteration:
                running.remove(chain)
    finish_grams(ITERS - 1)
    for b in range(inputs):
        for h in range(pieces):
            own = image[b, ITERS - 1, h].reshape(rank, piece)
            out_ref[b * rank:(b + 1) * rank, h * piece:(h + 1) * piece] = apply_inverse(inverses[ITERS - 1][b], own)
    for condition, copy in pending:
        if condition is None:
            copy.wait_send()
        else:
            @pl.when(condition)
            def _():
                copy.wait_send()


def on_device(rows, cols, slices, weights, preact, panel):
    layers, out_block, in_block = weights.shape
    inputs, rank, _ = panel.shape
    per, pieces = rows // cols, rows // slices
    vm = pltpu.VMEM
    dma = pltpu.SemaphoreType.DMA
    many = (inputs, ITERS, layers)
    once = (inputs, ITERS)
    by_col = (cols, rank // cols, out_block)
    by_row = (pieces, slices, rank // slices, in_block // pieces)
    scratch = [
        vm((layers, out_block, in_block), BF16),
        vm((inputs * layers, out_block), F32),
        vm(many + by_col, BF16),
        vm(many + by_col, BF16),
        vm(many + (rows, rank // cols, out_block), BF16),
        vm(many + (per,) + by_col, BF16),
        vm(many + by_col, BF16),
        vm(many + (cols, per, rank // cols, out_block), BF16),
        vm(many + (cols, per, rank // cols, out_block), BF16),
        vm(many + (rows, rank // cols, out_block), BF16),
        vm(many + (rank, out_block), BF16),
        vm(once + by_row, BF16),
        vm(once + by_row, BF16),
        vm(once + by_row, BF16),
        vm(once + (cols, rank, 2 * rank), F32),
        dma((layers,)),
        dma(once + (3 * layers + 1, cols)), dma(once + (3 * layers + 1, cols)),
        dma(once + (layers + 2, rows)), dma(once + (layers + 2, rows)),
        dma(many + (rows,)), dma(many + (per, cols)),
        dma(many + (rows,)), dma(many + (rows,)),
    ]
    whole = pl.BlockSpec(memory_space=pltpu.VMEM)
    out = pl.pallas_call(
        partial(kernel, rows, cols, inputs, rank, out_block, in_block, slices),
        out_shape=jax.ShapeDtypeStruct((inputs * rank, in_block), F32),
        in_specs=[pl.BlockSpec(memory_space=pl.ANY), whole, whole],
        out_specs=whole,
        scratch_shapes=scratch,
        compiler_params=pltpu.CompilerParams(
            collective_id=0, has_side_effects=True, vmem_limit_bytes=56 * 1024 * 1024),
    )(weights, preact.reshape(inputs * layers, out_block), panel.reshape(inputs * rank, in_block))
    return out.reshape(inputs, rank, in_block)


def solution(mesh):
    rows, cols = mesh.shape["row"], mesh.shape["col"]

    def body(weights, preact, panel):
        layers, out_block, in_block = weights.shape
        inputs, rank, _ = panel.shape
        slices = max(rank // 16, 1)
        fits = (
            rows % cols == 0 and rows * out_block == cols * in_block and out_block % 256 == 0
            and rank % (16 * cols) == 0 and rows % slices == 0 and in_block % (256 * (rows // slices)) == 0
        )
        if fits:
            return on_device(rows, cols, slices, weights, preact, panel)
        return plain_on_device(weights, preact, panel)

    return jax.shard_map(
        body,
        mesh=mesh,
        in_specs=(P(None, "row", "col"), P(None, None, "row"), P(None, None, "col")),
        out_specs=P(None, None, "col"),
        check_vma=False,
    )
```

```python
from functools import partial

import jax
import jax.numpy as jnp
from jax import lax
from jax.experimental import pallas as pl
from jax.experimental.pallas import tpu as pltpu
from jax.sharding import PartitionSpec as P

ITERS = 2
MESH = pl.DeviceIdType.MESH
F32, BF16 = jnp.float32, jnp.bfloat16


def plain_on_device(weights, preact, panel):
    width = panel.shape[2] * lax.axis_size("col")
    slopes = 1.0 - jnp.tanh(preact) ** 2
    layers = weights.shape[0]
    current = panel
    basis_out = panel.astype(F32)
    for iteration in range(ITERS):
        cotangent = None
        for layer_at in range(layers):
            partial_out = jnp.einsum("bki,oi->bko", current, weights[layer_at], preferred_element_type=F32)
            summed = lax.psum_scatter(
                partial_out.astype(BF16), "col", scatter_dimension=1, tiled=True
            ).astype(F32)
            scaled = (slopes[:, layer_at, None, :] * summed).astype(BF16)
            if layer_at + 1 < layers:
                spread = lax.all_gather(scaled, "row", axis=2, tiled=True)
                current = lax.all_to_all(spread, "col", split_axis=2, concat_axis=1, tiled=True)
            else:
                cotangent = lax.all_gather(scaled, "col", axis=1, tiled=True)
        image_panel = None
        for layer_at in reversed(range(layers)):
            weighted = (slopes[:, layer_at, None, :] * cotangent).astype(BF16)
            partial_in = jnp.einsum("bko,oi->bki", weighted, weights[layer_at], preferred_element_type=F32)
            if layer_at == 0:
                pieces = lax.psum_scatter(partial_in.astype(BF16), "row", scatter_dimension=2, tiled=True)
                image_panel = lax.all_gather(pieces, "row", axis=2, tiled=True)
            else:
                pieces = lax.psum_scatter(partial_in.astype(BF16), "row", scatter_dimension=1, tiled=True)
                spread = lax.all_gather(pieces, "col", axis=2, tiled=True)
                cotangent = lax.all_to_all(spread, "row", split_axis=2, concat_axis=1, tiled=True)
        local_gram = jnp.einsum("bkw,bjw->bkj", image_panel, image_panel, preferred_element_type=F32)
        gram_sum = lax.psum(local_gram.astype(BF16), "col").astype(F32)
        factor = jnp.linalg.cholesky(gram_sum / width)
        basis_out = jax.vmap(partial(jax.scipy.linalg.solve_triangular, lower=True))(
            factor, image_panel.astype(F32)
        )
        current = basis_out.astype(BF16)
    return basis_out


def inverse_factors(gram, inputs, rank, width):
    at_row = lax.broadcasted_iota(jnp.int32, (rank, 1), 0)
    row_at = lax.broadcasted_iota(jnp.int32, (rank, rank), 0)
    col_at = lax.broadcasted_iota(jnp.int32, (rank, rank), 1)
    eye = (row_at == col_at).astype(F32)
    joined = [
        jnp.concatenate([gram[:, b * rank:(b + 1) * rank], eye], axis=1) for b in range(inputs)
    ]
    for k in range(rank):
        for b in range(inputs):
            now = joined[b]
            pivot_row = now[k:k + 1, :]
            share = now[:, k:k + 1] / now[k:k + 1, k:k + 1]
            joined[b] = now - jnp.where(at_row > k, share, 0.0) * pivot_row
    inverses = []
    for b in range(inputs):
        diagonal = jnp.sum(joined[b][:, :rank] * eye, axis=1, keepdims=True)
        inverses.append(joined[b][:, rank:] * jnp.sqrt(width / diagonal))
    return inverses


def apply_inverse(inverse, panel):
    high = inverse.astype(BF16)
    low = (inverse - high.astype(F32)).astype(BF16)
    return jnp.dot(high, panel, preferred_element_type=F32) + jnp.dot(low, panel, preferred_element_type=F32)


def kernel(
    rows, cols, inputs, rank, out_block, in_block, slices,
    w_hbm, preact_ref, panel_ref, out_ref,
    w, slopes, part_col, got_col, ring, spread, gathered_col, part_in, traded, summed_in, weighted,
    pair_in, send_in, part_row, pair_row, send_row, got_row, image, gram, w_sem, col_send, col_recv, row_send, row_recv,
    fwd_send, fwd_recv, sum_send, sum_recv,
):
    r, c = lax.axis_index("row"), lax.axis_index("col")
    layers = w.shape[0]
    per = rows // cols
    k_col, k_row = rank // cols, rank // slices
    pieces = rows // slices
    piece = in_block // pieces
    width = cols * in_block
    tile = 256

    loads = [pltpu.make_async_copy(w_hbm.at[l], w.at[l], w_sem.at[l]) for l in range(layers)]
    for load in loads:
        load.start()
    barrier = pltpu.get_barrier_semaphore()
    for d in range(1, rows):
        pl.semaphore_signal(barrier, inc=1, device_id={"row": lax.rem(r + d, rows)}, device_id_type=MESH)
    for d in range(1, cols):
        pl.semaphore_signal(barrier, inc=1, device_id={"col": lax.rem(c + d, cols)}, device_id_type=MESH)
    slopes[...] = 1.0 - jnp.tanh(preact_ref[...]) ** 2
    pl.semaphore_wait(barrier, rows + cols - 2)

    major, minor = r // per, lax.rem(r, per)

    def push(source, place, send, recv, row, condition=None):
        copy = pltpu.make_async_remote_copy(
            src_ref=source, dst_ref=place, send_sem=send, recv_sem=recv,
            device_id={"row": row}, device_id_type=MESH)
        if condition is None:
            copy.start()
        else:
            @pl.when(condition)
            def _():
                copy.start()
        pending.append((condition, copy))

    def landed(place, send, recv):
        pltpu.make_async_remote_copy(
            src_ref=place, dst_ref=place, send_sem=send, recv_sem=recv,
            device_id={"row": r}, device_id_type=MESH).wait_recv()

    def spread_rows(shard, send, recv, each=None):
        for d in range(1, cols):
            push(shard(r), shard(r), send.at[d], recv.at[d], lax.rem(major + d, cols) * per + minor)
        for d in range(cols):
            if d == 1:
                yield
            source = lax.rem(major + cols - d, cols) * per + minor
            if d:
                landed(shard(source), send.at[d], recv.at[d])
            for e in range(1, per):
                at = cols + d * per + e
                push(shard(source), shard(source), send.at[at], recv.at[at], major * per + lax.rem(minor + e, per))
            if each:
                each(d * per, source)
        yield
        for d in range(cols):
            for e in range(1, per):
                at = cols + d * per + e
                source = lax.rem(major + cols - d, cols) * per + lax.rem(minor + per - e, per)
                landed(shard(source), send.at[at], recv.at[at])
                if each:
                    each(d * per + e, source)

    pending = []
    loaded = set()
    gram_arrivals = []
    inverses = {}

    def need(layer):
        if layer not in loaded:
            loaded.add(layer)
            loads[layer].wait()

    def trade(axis, source_of, place_of, send, recv):
        me, size = (r, rows) if axis == "row" else (c, cols)
        for d in range(1, size):
            peer = lax.rem(me + d, size)
            copy = pltpu.make_async_remote_copy(
                src_ref=source_of(peer), dst_ref=place_of(me), send_sem=send.at[d], recv_sem=recv.at[d],
                device_id={axis: peer}, device_id_type=MESH)
            copy.start()
            pending.append((None, copy))

        def arrive(d):
            origin = lax.rem(me + size - d, size)
            pltpu.make_async_remote_copy(
                src_ref=source_of(origin), dst_ref=place_of(origin), send_sem=send.at[d], recv_sem=recv.at[d],
                device_id={axis: origin}, device_id_type=MESH).wait_recv()
            return origin

        return arrive

    def forward(layer, lhs, into):
        need(layer)

        def step(t, carry):
            at = pl.ds(pl.multiple_of(t * tile, tile), tile)
            total = None
            for value, low, high in lhs():
                term = lax.dot_general(
                    value, w[layer, at, low:high], (((1,), (1,)), ((), ())), preferred_element_type=F32)
                total = term if total is None else total + term
            into[:, :, at] = total.astype(BF16).reshape(cols, k_col, tile)
            return carry
        lax.fori_loop(0, out_block // tile, step, 0)

    def backward(layer, lhs_ref, store):
        def step(t, carry):
            at = pl.ds(pl.multiple_of(t * tile, tile), tile)
            store(t, jnp.dot(lhs_ref[...], w[layer, :, at], preferred_element_type=F32).astype(BF16))
            return carry
        lax.fori_loop(0, in_block // tile, step, 0)

    def stream(b):
        for it in range(ITERS):
            if it == 0:
                lhs = lambda: [(panel_ref[b * rank:(b + 1) * rank, :], 0, in_block)]
            else:
                lhs = lambda: [
                    (image[b, it - 1, h].reshape(rank, piece), h * piece, (h + 1) * piece) for h in range(pieces)]
            for layer in range(layers):
                slope = slopes[b * layers + layer:b * layers + layer + 1, :]
                part, got = part_col.at[b, it, layer], got_col.at[b, it, layer]
                forward(layer, lhs, part)
                arrive = trade("col", lambda peer: part.at[peer], lambda me: got.at[me],
                               col_send.at[b, it, layer], col_recv.at[b, it, layer])
                yield
                total = part[c].astype(F32)
                for d in range(1, cols):
                    total = total + got[arrive(d)].astype(F32)
                if layer + 1 < layers:
                    shards, blocks = ring.at[b, it, layer], spread.at[b, it, layer]
                    shards[r] = (slope * total).astype(BF16)

                    def pass_on(d, origin):
                        owner, at = origin // per, lax.rem(origin, per)
                        copy = pltpu.make_async_remote_copy(
                            src_ref=shards.at[origin], dst_ref=blocks.at[at, c],
                            send_sem=fwd_send.at[b, it, layer, d], recv_sem=fwd_recv.at[b, it, layer, at, c],
                            device_id={"col": owner}, device_id_type=MESH)

                        @pl.when(owner != c)
                        def _():
                            copy.start()

                        @pl.when(owner == c)
                        def _():
                            blocks[at, c] = shards[origin]
                        pending.append((owner != c, copy))

                    steps = spread_rows(
                        lambda at: shards.at[at], row_send.at[b, it, layer], row_recv.at[b, it, layer], pass_on)
                    next(steps)
                    if it > 0 and layer == 0 and b == inputs - 1:
                        finish_grams(it - 1)
                    yield
                    yield from steps
                    yield
                    for at in range(per):
                        for d in range(1, cols):
                            origin = lax.rem(c + d, cols)
                            pltpu.make_async_remote_copy(
                                src_ref=blocks.at[at, origin], dst_ref=blocks.at[at, origin],
                                send_sem=fwd_send.at[b, it, layer, 0], recv_sem=fwd_recv.at[b, it, layer, at, origin],
                                device_id={"col": origin}, device_id_type=MESH).wait_recv()
                    lhs = lambda blocks=blocks: [
                        (blocks[at].reshape(rank, out_block), at * out_block, (at + 1) * out_block)
                        for at in range(per)]
                else:
                    cot = gathered_col.at[b, it, layer]
                    cot[c] = ((slope * total) if it == 0 else total).astype(BF16)
                    arrive = trade("col", lambda peer: cot.at[c], lambda me: cot.at[me],
                                   col_send.at[b, it, layers], col_recv.at[b, it, layers])
                    yield
                    for d in range(1, cols):
                        arrive(d)
            for layer in reversed(range(layers)):
                slope = slopes[b * layers + layer:b * layers + layer + 1, :]
                scaled = weighted.at[b, it, layer]
                value = cot[...].reshape(rank, out_block)
                if layer == layers - 1 and it > 0:
                    value = (slope * apply_inverse(inverses[it - 1][b], value)).astype(BF16)
                scaled[...] = (slope * value.astype(F32)).astype(BF16)
                if layer > 0:
                    whole, slots = traded.at[b, it, layer], summed_in.at[b, it, layer]
                    source = part_in.at[b, it, layer]

                    def store(t, value):
                        ratio = out_block // tile
                        at = pl.ds(pl.multiple_of(lax.rem(t, ratio) * tile, tile), tile)
                        source[:, t // ratio, :, at] = value.reshape(cols, k_col, tile)
                    backward(layer, scaled, store)
                    arrive = trade("col", lambda peer: source.at[peer], lambda me: whole.at[me],
                                   col_send.at[b, it, layers + layer], col_recv.at[b, it, layers + layer])
                    whole[c] = source[c]
                    yield
                    pair, ready = pair_in.at[b, it, layer], send_in.at[b, it, layer]
                    send, recv = sum_send.at[b, it, layer], sum_recv.at[b, it, layer]
                    for d in range(cols):
                        owner = arrive(d) if d else c
                        for e in range(1, per):
                            peer = lax.rem(minor + e, per)
                            push(whole.at[owner, peer], pair.at[owner, e], send.at[d * per + e], recv.at[d * per + e],
                                 major * per + peer)
                    yield
                    for d in range(cols):
                        owner = lax.rem(c + cols - d, cols)
                        total = whole[owner, minor].astype(F32)
                        for e in range(1, per):
                            landed(pair.at[owner, e], send.at[d * per + e], recv.at[d * per + e])
                            total = total + pair[owner, e].astype(F32)
                        ready[owner] = total.astype(BF16)
                        push(ready.at[owner], slots.at[major], send.at[rows + d], recv.at[rows + major],
                             owner * per + minor, owner != major)
                    yield
                    total = whole[major, minor].astype(F32)
                    for e in range(1, per):
                        total = total + pair[major, e].astype(F32)
                    for d in range(1, cols):
                        origin = lax.rem(major + d, cols)
                        landed(slots.at[origin], send.at[rows], recv.at[rows + origin])
                        total = total + slots[origin].astype(F32)
                    cot = gathered_col.at[b, it, layer - 1]
                    cot[c] = total.astype(BF16)
                    arrive = trade("col", lambda peer: cot.at[c], lambda me: cot.at[me],
                                   col_send.at[b, it, 2 * layers + layer - 1],
                                   col_recv.at[b, it, 2 * layers + layer - 1])
                    yield
                    for d in range(1, cols):
                        arrive(d)
                else:
                    mine, got, final = part_row.at[b, it], got_row.at[b, it], image.at[b, it]

                    def store(t, value):
                        ratio = piece // tile
                        at = pl.ds(pl.multiple_of(lax.rem(t, ratio) * tile, tile), tile)
                        mine[t // ratio, :, :, at] = value.reshape(slices, k_row, tile)
                    backward(layer, scaled, store)

                    def shard(ref):
                        return lambda at: ref.at[at // slices, lax.rem(at, slices)]
                    pair, ready = pair_row.at[b, it], send_row.at[b, it]
                    send, recv = row_send.at[b, it, layers], row_recv.at[b, it, layers]
                    order = list(range(1, cols)) + [0]
                    for d in order:
                        to = lax.rem(major + d, cols)
                        for e in range(1, per):
                            peer = lax.rem(minor + e, per)
                            push(shard(mine)(to * per + peer), pair.at[to, e], send.at[d * per + e],
                                 recv.at[d * per + e], major * per + peer)
                    yield
                    for d in order:
                        to = lax.rem(major + d, cols)
                        total = shard(mine)(to * per + minor)[...].astype(F32)
                        for e in range(1, per):
                            landed(pair.at[to, e], send.at[d * per + e], recv.at[d * per + e])
                            total = total + pair[to, e].astype(F32)
                        if d:
                            ready[to] = total.astype(BF16)
                            push(ready.at[to], got.at[major], send.at[rows + d], recv.at[rows + d], to * per + minor)
                    yield
                    for d in range(1, cols):
                        origin = lax.rem(major + cols - d, cols)
                        landed(got.at[origin], send.at[rows + d], recv.at[rows + d])
                        total = total + got[origin].astype(F32)
                    shard(final)(r)[...] = total.astype(BF16)
                    yield from spread_rows(
                        shard(final), row_send.at[b, it, layers + 1], row_recv.at[b, it, layers + 1])
            local = None
            for h in range(pieces):
                own = image[b, it, h].reshape(rank, piece)
                term = lax.dot_general(own, own, (((1,), (1,)), ((), ())), preferred_element_type=F32)
                local = term if local is None else local + term
            here = gram.at[b, it]
            here[c] = jnp.concatenate([local, local], axis=1)
            gram_arrivals.append((it, b, trade(
                "col", lambda peer, here=here: here.at[c], lambda me, here=here: here.at[me],
                col_send.at[b, it, 3 * layers], col_recv.at[b, it, 3 * layers])))

    def finish_grams(it):
        totals = {}
        for at, b, arrive in gram_arrivals:
            if at == it:
                for d in range(1, cols):
                    arrive(d)
                total = gram[b, it, 0]
                for d in range(1, cols):
                    total = total + gram[b, it, d]
                totals[b] = total[:, :rank]
        joint = jnp.concatenate([totals[b] for b in range(inputs)], axis=1)
        inverses[it] = inverse_factors(joint, inputs, rank, float(width))

    running = [stream(b) for b in range(inputs)]
    while running:
        for chain in list(running):
            try:
                next(chain)
            except StopIteration:
                running.remove(chain)
    finish_grams(ITERS - 1)
    for b in range(inputs):
        for h in range(pieces):
            own = image[b, ITERS - 1, h].reshape(rank, piece)
            out_ref[b * rank:(b + 1) * rank, h * piece:(h + 1) * piece] = apply_inverse(inverses[ITERS - 1][b], own)
    for condition, copy in pending:
        if condition is None:
            copy.wait_send()
        else:
            @pl.when(condition)
            def _():
                copy.wait_send()


def on_device(rows, cols, slices, weights, preact, panel):
    layers, out_block, in_block = weights.shape
    inputs, rank, _ = panel.shape
    per, pieces = rows // cols, rows // slices
    vm = pltpu.VMEM
    dma = pltpu.SemaphoreType.DMA
    many = (inputs, ITERS, layers)
    once = (inputs, ITERS)
    by_col = (cols, rank // cols, out_block)
    by_row = (pieces, slices, rank // slices, in_block // pieces)
    scratch = [
        vm((layers, out_block, in_block), BF16),
        vm((inputs * layers, out_block), F32),
        vm(many + by_col, BF16),
        vm(many + by_col, BF16),
        vm(many + (rows, rank // cols, out_block), BF16),
        vm(many + (per,) + by_col, BF16),
        vm(many + by_col, BF16),
        vm(many + (cols, per, rank // cols, out_block), BF16),
        vm(many + (cols, per, rank // cols, out_block), BF16),
        vm(many + by_col, BF16),
        vm(many + (rank, out_block), BF16),
        vm(many + (cols, per, rank // cols, out_block), BF16),
        vm(many + by_col, BF16),
        vm(once + by_row, BF16),
        vm(once + (cols, per) + by_row[2:], BF16),
        vm(once + (cols,) + by_row[2:], BF16),
        vm(once + (cols,) + by_row[2:], BF16),
        vm(once + by_row, BF16),
        vm(once + (cols, rank, 2 * rank), F32),
        dma((layers,)),
        dma(once + (3 * layers + 1, cols)), dma(once + (3 * layers + 1, cols)),
        dma(once + (layers + 2, rows + cols)), dma(once + (layers + 2, rows + cols)),
        dma(many + (rows,)), dma(many + (per, cols)),
        dma(many + (rows + cols,)), dma(many + (rows + cols,)),
    ]
    whole = pl.BlockSpec(memory_space=pltpu.VMEM)
    out = pl.pallas_call(
        partial(kernel, rows, cols, inputs, rank, out_block, in_block, slices),
        out_shape=jax.ShapeDtypeStruct((inputs * rank, in_block), F32),
        in_specs=[pl.BlockSpec(memory_space=pl.ANY), whole, whole],
        out_specs=whole,
        scratch_shapes=scratch,
        compiler_params=pltpu.CompilerParams(
            collective_id=0, has_side_effects=True, vmem_limit_bytes=56 * 1024 * 1024),
    )(weights, preact.reshape(inputs * layers, out_block), panel.reshape(inputs * rank, in_block))
    return out.reshape(inputs, rank, in_block)


def solution(mesh):
    rows, cols = mesh.shape["row"], mesh.shape["col"]

    def body(weights, preact, panel):
        layers, out_block, in_block = weights.shape
        inputs, rank, _ = panel.shape
        slices = max(rank // 16, 1)
        fits = (
            rows % cols == 0 and rows * out_block == cols * in_block and out_block % 256 == 0
            and rank % (16 * cols) == 0 and rows % slices == 0 and in_block % (256 * (rows // slices)) == 0
        )
        if fits:
            return on_device(rows, cols, slices, weights, preact, panel)
        return plain_on_device(weights, preact, panel)

    return jax.shard_map(
        body,
        mesh=mesh,
        in_specs=(P(None, "row", "col"), P(None, None, "row"), P(None, None, "col")),
        out_specs=P(None, None, "col"),
        check_vma=False,
    )
```
